32 devices in a mesh: heads: 2 (over y), ctx: 16 (over z, x, core).
Axes of the slice: x: 2, y: 2, z: 4, core: 2. Of those that a mesh axis runs over, the one named last changes fastest.
Arguments:
- queries: bfloat16 [8, 4096, 128], P('heads', 'ctx'), may hold values from -6 to 6
- key_rows: bfloat16 [8, 4096, 128], P('heads', 'ctx'), may hold values from -6 to 6
- value_rows: bfloat16 [8, 4096, 128], P('heads', 'ctx'), may hold values from -6 to 6
- level_weights: float32 [8, 13, 4096], P('heads', None, 'ctx'), may hold values from 0.1 to 3
- norm_gain: float32 [8, 128], P('heads'), may hold values from 0.1 to 1.9
- grad_normed: bfloat16 [8, 4096, 128], P('heads', 'ctx'), may hold values from -6 to 6
Outputs:
- normed: bfloat16 [8, 4096, 128], P('heads', 'ctx')
- grad_queries: bfloat16 [8, 4096, 128], P('heads', 'ctx')
- grad_keys: bfloat16 [8, 4096, 128], P('heads', 'ctx')
- grad_values: bfloat16 [8, 4096, 128], P('heads', 'ctx')
- grad_level_weights: float32 [8, 13, 4096], P('heads', None, 'ctx')
The draws below stay inside these ranges and needn't reach their ends.
All inputs are finite; a program needn't handle non-finite values.
Results may differ from the reference program's by a relative error of at most 0.006.
Values sent between devices are 32-bit elements; how exact they have to be, the bound alone decides.
A program may use at most 64 MiB of HBM per device.

```python
import math
import jax
import jax.numpy as jnp
from jax import lax

HD = 128
TOK_DEV = 256
HEADS = 8
TOKENS = 4096
LOCAL = 9
FAR = 4
LEVELS = 13
N_CTX = 16


def draw_level_weights(key, part):
    shape = (HEADS, LEVELS, TOKENS)
    head_pos = jnp.arange(HEADS, dtype=jnp.float32)
    rising = 1.0 + 2.0 * head_pos / max(HEADS - 1, 1)
    base = jnp.exp(jax.random.uniform(key, shape, jnp.float32, math.log(0.1), 0.0))
    return base * rising[:, None, None]


def block_levels(own_key, dims, pieces, least, high):
    factor_of = 1.0
    for dim, shards_of in pieces:
        steps = jax.random.uniform(jax.random.fold_in(jax.random.fold_in(own_key, 6), dim), (shards_of,), jnp.float32, least / len(pieces), high / len(pieces))
        factor_of = factor_of * jnp.repeat(jnp.exp(steps), dims[dim] // shards_of).reshape((-1,) + (1,) * (len(dims) - 1 - dim))
    return factor_of


def bell_draw(own_key, shape, deviation, reach, cuts=(), held_as=jnp.bfloat16):
    level = block_levels(own_key, shape, cuts, -0.22, 0.18) if cuts else 1.0
    result = jax.random.normal(own_key, shape, jnp.float32) * deviation * level
    return jnp.minimum(jnp.maximum(result, -reach), reach).astype(held_as)


def setup_inputs(seed: int = 0) -> dict:
    splits = jax.random.split(jax.random.key(seed), 7)
    queries = bell_draw(splits[0], (HEADS, TOKENS, HD), 1.0, 6.0, ((0, 2), (1, 16)))
    key_rows = bell_draw(splits[1], (HEADS, TOKENS, HD), 1.0, 6.0, ((0, 2), (1, 16)))
    value_rows = bell_draw(splits[2], (HEADS, TOKENS, HD), 1.0, 6.0, ((0, 2), (1, 16)))
    level_weights = draw_level_weights(jax.random.fold_in(splits[6], 71), 0)
    norm_gain = jnp.clip(1.0 + 0.18 * jax.random.normal(splits[4], (HEADS, HD), jnp.float32), 0.1, 1.9)
    grad_normed = bell_draw(splits[5], (HEADS, TOKENS, HD), 1.0, 6.0, ((0, 2), (1, 16)))
    return dict(queries=queries, key_rows=key_rows, value_rows=value_rows, level_weights=level_weights, norm_gain=norm_gain, grad_normed=grad_normed)


EPS = 1e-06
HIGH = lax.Precision.HIGHEST

def level_scale(number, head_dim):
    return 2.0 ** (-max(number - 1, 0) / 2.0) / math.sqrt(head_dim)

def level_matrix(count):
    position = jnp.arange(count, dtype=jnp.int32)
    differ = jnp.bitwise_xor(position[:, None], position[None, :])
    bucket = jnp.zeros((count, count), jnp.int32)
    for exponent in range(count.bit_length() - 1):
        bucket = bucket + (differ >= 2 ** exponent).astype(jnp.int32)
    causal = position[None, :] <= position[:, None]
    return (bucket, causal)

def near_weights(factors, bucket, causal, head_dim):
    weights = jnp.zeros(factors[0].shape + (bucket.shape[1],), jnp.float32)
    for number in range(len(factors)):
        scaled = factors[number] * level_scale(number, head_dim)
        weights = weights + jnp.where((bucket == number) & causal, scaled[..., None], jnp.float32(0.0))
    return weights

def far_states(key_value):
    stacked = []
    for depth in range(FAR):
        span = 2 ** depth
        group_sum = lax.optimization_barrier(jnp.sum(key_value.reshape(N_CTX // span, span, HD, HD), axis=1))
        before = jnp.concatenate([jnp.zeros((1, HD, HD), jnp.float32), group_sum[:-1]], 0)
        chosen = jnp.where((jnp.arange(N_CTX // span) % 2 == 1)[:, None, None], before, jnp.float32(0.0))
        stacked.append(jnp.repeat(chosen, span, axis=0))
    return jnp.stack(stacked, 0)

def back_states(grad_states):
    total = jnp.zeros((N_CTX, HD, HD), jnp.float32)
    for depth in range(FAR):
        span = 2 ** depth
        group_sum = lax.optimization_barrier(jnp.sum(grad_states[depth].reshape(N_CTX // span, span, HD, HD), axis=1))
        after = jnp.concatenate([group_sum[1:], jnp.zeros((1, HD, HD), jnp.float32)], 0)
        chosen = jnp.where((jnp.arange(N_CTX // span) % 2 == 0)[:, None, None], after, jnp.float32(0.0))
        total = total + jnp.repeat(chosen, span, axis=0)
    return total

def prepare(packed):
    query_head, key_head, value_head, rate_head = packed[:4]
    q_blocks = query_head.reshape(N_CTX, TOK_DEV, HD).astype(jnp.float32)
    k_blocks = key_head.reshape(N_CTX, TOK_DEV, HD).astype(jnp.float32)
    v_blocks = value_head.reshape(N_CTX, TOK_DEV, HD).astype(jnp.float32)
    rate_blocks = rate_head.reshape(LEVELS, N_CTX, TOK_DEV)
    key_value = jnp.einsum('nsd,nse->nde', k_blocks, v_blocks, precision=HIGH)
    states = far_states(key_value)
    bucket, causal = level_matrix(TOK_DEV)
    weights = near_weights([rate_blocks[number] for number in range(LOCAL)], bucket, causal, HD)
    scores = jnp.einsum('ntd,nsd->nts', q_blocks, k_blocks, precision=HIGH)
    weighted = lax.optimization_barrier((weights * scores).astype(jnp.bfloat16)).astype(jnp.float32)
    far_scale = jnp.stack([rate_blocks[LOCAL + depth] * level_scale(LOCAL + depth, HD) for depth in range(FAR)], 0)
    far_terms = jnp.einsum('ntd,mnde->mnte', q_blocks, states, precision=HIGH)
    return (q_blocks, k_blocks, v_blocks, states, bucket, causal, weights, scores, weighted, far_scale, far_terms)

def forward_head(packed):
    q_blocks, k_blocks, v_blocks, states, bucket, causal, weights, scores, weighted, far_scale, far_terms = prepare(packed)
    near_out = jnp.einsum('nts,nse->nte', weighted, v_blocks, precision=HIGH)
    attended = near_out + lax.optimization_barrier(jnp.sum(far_scale[..., None] * far_terms, 0))
    return attended.reshape(TOKENS, HD)

def backward_head(packed):
    q_blocks, k_blocks, v_blocks, states, bucket, causal, weights, scores, weighted, far_scale, far_terms = prepare(packed)
    grad_out = packed[4].reshape(N_CTX, TOK_DEV, HD).astype(jnp.float32)
    grad_mix = jnp.einsum('nte,nse->nts', grad_out, v_blocks, precision=HIGH)
    product = grad_mix * scores
    near_grads = [level_scale(number, HD) * lax.optimization_barrier(jnp.sum(jnp.where((bucket == number) & causal, product, jnp.float32(0.0)), axis=2)) for number in range(LOCAL)]
    far_grads = [level_scale(LOCAL + depth, HD) * lax.optimization_barrier(jnp.sum(grad_out * far_terms[depth], axis=2)) for depth in range(FAR)]
    grad_scores = lax.optimization_barrier((weights * grad_mix).astype(jnp.bfloat16)).astype(jnp.float32)
    grad_q = jnp.einsum('nts,nsd->ntd', grad_scores, k_blocks, precision=HIGH)
    grad_q = grad_q + lax.optimization_barrier(jnp.sum(far_scale[..., None] * jnp.einsum('nte,mnde->mntd', grad_out, states, precision=HIGH), 0))
    scaled_queries = lax.optimization_barrier((far_scale[..., None] * q_blocks[None]).astype(jnp.bfloat16)).astype(jnp.float32)
    grad_states = jnp.einsum('mntd,nte->mnde', scaled_queries, grad_out, precision=HIGH)
    grad_kv = lax.optimization_barrier(back_states(grad_states).astype(jnp.bfloat16)).astype(jnp.float32)
    grad_k = jnp.einsum('nts,ntd->nsd', grad_scores, q_blocks, precision=HIGH) + jnp.einsum('nse,nde->nsd', v_blocks, grad_kv, precision=HIGH)
    grad_v = jnp.einsum('nts,nte->nse', weighted, grad_out, precision=HIGH) + jnp.einsum('nsd,nde->nse', k_blocks, grad_kv, precision=HIGH)
    grad_rates = jnp.stack(near_grads + far_grads, 0).reshape(LEVELS, TOKENS)
    return (grad_q.reshape(TOKENS, HD).astype(jnp.bfloat16), grad_k.reshape(TOKENS, HD).astype(jnp.bfloat16), grad_v.reshape(TOKENS, HD).astype(jnp.bfloat16), grad_rates)

def reference(queries, key_rows, value_rows, level_weights, norm_gain, grad_normed):
    attended = lax.map(forward_head, (queries, key_rows, value_rows, level_weights))
    width = HEADS * HD
    totals = lax.optimization_barrier(jnp.sum(attended * attended, axis=(0, 2)))
    inv_rms = lax.rsqrt(totals / width + EPS)
    normed = (attended * inv_rms[None, :, None] * norm_gain[:, None, :]).astype(jnp.bfloat16)
    scaled = norm_gain[:, None, :] * grad_normed.astype(jnp.float32)
    inner_sum = lax.optimization_barrier(jnp.sum(scaled * attended, axis=(0, 2)))
    grad_out = (inv_rms[None, :, None] * scaled - attended * (inv_rms ** 3 * inner_sum / width)[None, :, None]).astype(jnp.bfloat16)
    grad_q, grad_k, grad_v, grad_rates = lax.map(backward_head, (queries, key_rows, value_rows, level_weights, grad_out))
    return (normed, grad_q, grad_k, grad_v, grad_rates)
```

```python
import functools
import math

import jax
import jax.numpy as jnp
from jax import lax
from jax.experimental import pallas as pl
from jax.experimental.pallas import tpu as pltpu
from jax.sharding import PartitionSpec as P

EPS = 1e-06
MESH = pl.DeviceIdType.MESH
F32 = jnp.float32
BF16 = jnp.bfloat16


def level_scale(number, head_dim):
    return 2.0 ** (-max(number - 1, 0) / 2.0) / math.sqrt(head_dim)


def dot(a, b):
    return jnp.dot(a, b, preferred_element_type=F32)


def dot_nt(a, b):
    return lax.dot_general(a, b, (((1,), (1,)), ((), ())), preferred_element_type=F32)


def kernel(
    n_ctx, n_heads, chunks,
    q_ref, k_ref, v_ref, lw_ref, gain_ref, gn_ref,
    normed_ref, gq_ref, gk_ref, gv_ref, glw_ref,
    bucket_ref, qt_ref, scores_ref, weights_ref, weighted_ref, sq_ref, att_ref, scaled_ref, gt_ref,
    states_ref, gk_acc, gv_acc,
    gsum, rcv, gs, rs, tx, brcv, abuf, hx, hx_in,
    fs_sem, fr_sem, gas_sem, gar_sem, rss_sem, rsr_sem, bs_sem, br_sem, hs_sem, hr_sem,
):
    heads, tokens, dim = q_ref.shape
    far = n_ctx.bit_length() - 1
    local = tokens.bit_length()
    width = heads * n_heads * dim
    rows = heads * dim
    part = rows // chunks
    per_chunk = heads // chunks
    me = lax.axis_index("ctx")
    mine = lax.axis_index("heads")
    bits = [(me // 2**i) % 2 for i in range(far)]

    def peer(j):
        other = me
        for i in range(far):
            if j >> i & 1:
                other = other + (1 - 2 * bits[i]) * 2**i
        return other

    def peer_bits(j):
        return [1 - bits[i] if j >> i & 1 else bits[i] for i in range(far)]

    def place(which, m, c):
        start = c * part
        for i in range(m):
            start = start + which[i] * (part >> (i + 1))
        return start

    def span(start, size):
        return pl.ds(pl.multiple_of(start, 8), size)

    barrier = pltpu.get_barrier_semaphore()
    friends = list(range(1, n_ctx // 2)) + [n_ctx // 2]
    for j in friends:
        pl.semaphore_signal(barrier, inc=1, device_id={"ctx": peer(j)}, device_id_type=MESH)
    for j in range(1, n_heads):
        pl.semaphore_signal(
            barrier, inc=1, device_id={"heads": (mine + j) % n_heads}, device_id_type=MESH
        )

    def key_value(h):
        gsum[0, h * dim : (h + 1) * dim, :] = dot(k_ref[h].T, v_ref[h])

    def remote(src, dst, ssem, rsem, target, axis="ctx"):
        return pltpu.make_async_remote_copy(
            src_ref=src, dst_ref=dst, send_sem=ssem, recv_sem=rsem,
            device_id={axis: target}, device_id_type=MESH,
        )

    def fwd_copy(m, c):
        where = span(place(bits, m, c), part >> m)
        return remote(
            gsum.at[m, where, :], rcv.at[m, where, :], fs_sem.at[m, c], fr_sem.at[m, c], peer(2**m)
        )

    def gather_copies(m, c):
        where = span(place(bits, m, c), part >> m)
        return [
            remote(rcv.at[m, where, :], rcv.at[m, where, :], gas_sem.at[m, c], gar_sem.at[m, c], peer(j))
            for j in range(1, 2**m)
        ]

    def fwd_step(m, c):
        fwd_copy(m, c).wait_recv()
        if m < far - 1:
            half = span(place(bits, m + 1, c), part >> (m + 1))
            gsum[m + 1, half, :] = gsum[m, half, :] + rcv[m, half, :]
            fwd_copy(m + 1, c).start()
        if m > 0:

            @pl.when(bits[m] == 1)
            def _():
                for copy in gather_copies(m, c):
                    copy.start()

    def gather_rows(m):
        return part - (part >> m)

    def local_wait(buffer, count, sem):
        pltpu.make_async_copy(buffer.at[pl.ds(0, count), :], buffer.at[pl.ds(0, count), :], sem).wait()

    s_pos = lax.broadcasted_iota(jnp.int32, (tokens, tokens), 0)
    t_pos = lax.broadcasted_iota(jnp.int32, (tokens, tokens), 1)

    def make_bucket():
        differ = jnp.bitwise_xor(s_pos, t_pos)
        bucket = jnp.zeros((tokens, tokens), jnp.int32)
        for exponent in range(local - 1):
            bucket = bucket + (differ >= 2**exponent).astype(jnp.int32)
        bucket_ref[...] = jnp.where(s_pos <= t_pos, bucket, -1)

    def near_forward(h):
        q_t = q_ref[h].T
        qt_ref[h] = q_t
        scores = dot(k_ref[h], q_t)
        scores_ref[h] = scores
        bucket = bucket_ref[...]
        weights = jnp.zeros((tokens, tokens), F32)
        for number in range(local):
            row = lw_ref[h, number : number + 1, :] * level_scale(number, dim)
            weights = jnp.where(bucket == number, row, weights)
        weights_ref[h] = weights
        weighted = (weights * scores).astype(BF16)
        weighted_ref[h] = weighted
        q_wide = q_t.astype(F32)
        for m in range(far):
            row = lw_ref[h, local + m : local + m + 1, :] * level_scale(local + m, dim)
            sq_ref[h, m * dim : (m + 1) * dim, :] = (row * q_wide).astype(BF16)
        att_ref[h] = dot(v_ref[h].T, weighted)
        gain = jnp.broadcast_to(gain_ref[h : h + 1, :], (tokens, dim))
        scaled_ref[h] = (gain * gn_ref[h].astype(F32)).T

    for h in range(per_chunk):
        key_value(h)
    pl.semaphore_wait(barrier, len(friends) + n_heads - 1)
    for c in range(chunks):
        if c > 0:
            for h in range(c * per_chunk, (c + 1) * per_chunk):
                key_value(h)
        fwd_copy(0, c).start()
    make_bucket()
    pending = list(range(heads))
    near_forward(pending.pop(0))
    for t in range(far + chunks - 1):
        for c in range(chunks):
            if 0 <= t - c < far:
                fwd_step(t - c, c)
        if pending:
            near_forward(pending.pop(0))
    while pending:
        near_forward(pending.pop(0))
    for m in range(far):

        @pl.when(bits[m] == 1)
        def _():
            for c in range(chunks):
                if m > 0:
                    local_wait(rcv.at[m], gather_rows(m), gar_sem.at[m, c])
            for h in range(heads):
                states_ref[h, m * dim : (m + 1) * dim, :] = rcv[m, h * dim : (h + 1) * dim, :].astype(BF16)

        @pl.when(bits[m] == 0)
        def _():
            for h in range(heads):
                states_ref[h, m * dim : (m + 1) * dim, :] = jnp.zeros((dim, dim), BF16)

    total = jnp.zeros((1, tokens), F32)
    inner = jnp.zeros((1, tokens), F32)
    for h in range(heads):
        att = att_ref[h] + dot(states_ref[h].T, sq_ref[h])
        att_ref[h] = att
        total = total + jnp.sum(att * att, axis=0, keepdims=True)
        inner = inner + jnp.sum(att * scaled_ref[h], axis=0, keepdims=True)
    hx[0:1, :] = total
    hx[1:2, :] = inner
    head_copies = [
        remote(hx, hx_in.at[j], hs_sem.at[j], hr_sem.at[j], (mine + j) % n_heads, "heads")
        for j in range(1, n_heads)
    ]
    for copy in head_copies:
        copy.start()
    for j, copy in enumerate(head_copies):
        copy.wait_recv()
        total = total + hx_in[j + 1, 0:1, :]
        inner = inner + hx_in[j + 1, 1:2, :]
    inv_rms = lax.rsqrt(total / width + EPS)
    pull = inv_rms * inv_rms * inv_rms * inner / width

    def scatter_copies(m, c):
        size = part >> m
        copies = []
        for j in range(1, 2**m):
            where = span(place(peer_bits(j), m, c), size)
            slot = pl.ds(j * chunks * size + c * size, size)
            copies.append(
                remote(gs.at[m, where, :], rs.at[m, slot, :], rss_sem.at[m, c], rsr_sem.at[m, c], peer(j))
            )
        return copies

    def up_copy(m, c):
        where = span(place(bits, m, c), part >> m)
        return remote(tx.at[m, where, :], brcv.at[m, where, :], bs_sem.at[m, c], br_sem.at[m, c], peer(2**m))

    def down_copy(m, c):
        where = span(place(bits[:m] + [0], m + 1, c), part >> (m + 1))
        return remote(
            abuf.at[m + 1, where, :], brcv.at[m, where, :], bs_sem.at[m, c], br_sem.at[m, c], peer(2**m)
        )

    def bwd_send(m, c):
        size = part >> m

        @pl.when(bits[m] == 1)
        def _():
            where = span(place(bits, m, c), size)
            sums = gs[m, where, :]
            if m > 0:
                local_wait(rs.at[m], gather_rows(m), rsr_sem.at[m, c])
                for j in range(1, 2**m):
                    slot = j * chunks * size + c * size
                    sums = sums + rs[m, slot : slot + size, :]
            tx[m, where, :] = sums
            if m < far - 1:
                half = span(place(bits[:m] + [1], m + 1, c), size // 2)
                tx[m, half, :] = tx[m, half, :] + abuf[m + 1, half, :]
            up_copy(m, c).start()

        if m < far - 1:

            @pl.when(bits[m] == 0)
            def _():
                down_copy(m, c).start()

    def bwd_recv(m, c):
        size = part >> m
        half0 = span(place(bits[:m] + [0], m + 1, c), size // 2)
        half1 = span(place(bits[:m] + [1], m + 1, c), size // 2)

        @pl.when(bits[m] == 0)
        def _():
            up_copy(m, c).wait_recv()
            low = brcv[m, half0, :]
            if m < far - 1:
                low = low + abuf[m + 1, half0, :]
            abuf[m, half0, :] = low
            abuf[m, half1, :] = brcv[m, half1, :]

        @pl.when(bits[m] == 1)
        def _():
            if m < far - 1:
                down_copy(m, c).wait_recv()
                abuf[m, half0, :] = brcv[m, half0, :]
                abuf[m, half1, :] = abuf[m + 1, half1, :]
            else:
                abuf[m, half0, :] = jnp.zeros((size // 2, dim), F32)
                abuf[m, half1, :] = jnp.zeros((size // 2, dim), F32)

    for c in range(chunks):
        for h in range(c * per_chunk, (c + 1) * per_chunk):
            g_t = (inv_rms * scaled_ref[h] - att_ref[h] * pull).astype(BF16)
            gt_ref[h] = g_t
            grads = dot_nt(sq_ref[h], g_t)
            for m in range(far):
                gs[m, h * dim : (h + 1) * dim, :] = grads[m * dim : (m + 1) * dim, :]
        for m in reversed(range(1, far)):

            @pl.when(bits[m] == 1)
            def _():
                for copy in scatter_copies(m, c):
                    copy.start()

    def near_backward(h):
        gain = jnp.broadcast_to(gain_ref[h : h + 1, :], (tokens, dim))
        normed_ref[h] = ((att_ref[h] * inv_rms).T * gain).astype(BF16)
        g_t = gt_ref[h]
        mix = dot(v_ref[h], g_t)
        grad_scores = (weights_ref[h] * mix).astype(BF16)
        product = mix * scores_ref[h]
        bucket = bucket_ref[...]
        for number in range(local):
            kept = jnp.where(bucket == number, product, 0.0)
            glw_ref[h, number : number + 1, :] = level_scale(number, dim) * jnp.sum(kept, axis=0, keepdims=True)
        grad_q = dot(k_ref[h].T, grad_scores)
        turned = dot(states_ref[h], g_t)
        q_wide = qt_ref[h].astype(F32)
        for m in range(far):
            block = turned[m * dim : (m + 1) * dim, :]
            scale = level_scale(local + m, dim)
            glw_ref[h, local + m : local + m + 1, :] = scale * jnp.sum(block * q_wide, axis=0, keepdims=True)
            grad_q = grad_q + (lw_ref[h, local + m : local + m + 1, :] * scale) * block
        gq_ref[h] = grad_q.T.astype(BF16)
        gk_acc[h] = dot_nt(grad_scores, qt_ref[h])
        gv_acc[h] = dot_nt(weighted_ref[h], g_t)

    pending = list(range(heads))
    near_backward(pending.pop(0))
    for t in range(far + chunks):
        for c in range(chunks):
            stage = t - c
            if 1 <= stage <= far:
                bwd_recv(far - stage, c)
                if stage == far:
                    for h in range(c * per_chunk, (c + 1) * per_chunk):
                        while h in pending:
                            near_backward(pending.pop(0))
                        grad_kv = abuf[0, h * dim : (h + 1) * dim, :].astype(BF16)
                        gk_ref[h] = (gk_acc[h] + dot_nt(v_ref[h], grad_kv)).astype(BF16)
                        gv_ref[h] = (gv_acc[h] + dot(k_ref[h], grad_kv)).astype(BF16)
            if 0 <= stage < far:
                bwd_send(far - 1 - stage, c)
        if pending:
            near_backward(pending.pop(0))

    for copy in head_copies:
        copy.wait_send()
    for c in range(chunks):
        for m in range(far):
            fwd_copy(m, c).wait_send()

            @pl.when(bits[m] == 1)
            def _():
                if m > 0:
                    local_wait(rcv.at[m], gather_rows(m), gas_sem.at[m, c])
                    local_wait(gs.at[m], gather_rows(m), rss_sem.at[m, c])
                up_copy(m, c).wait_send()

            if m < far - 1:

                @pl.when(bits[m] == 0)
                def _():
                    down_copy(m, c).wait_send()


def shards(n_ctx, n_heads, queries, key_rows, value_rows, level_weights, norm_gain, grad_normed):
    heads, tokens, dim = queries.shape
    far = n_ctx.bit_length() - 1
    rows = heads * dim
    chunks = max(c for c in (1, 2, 4) if heads % c == 0 and rows // c >> (far - 1) >= 16)
    vmem = pl.BlockSpec(memory_space=pltpu.VMEM)
    square = (heads, tokens, tokens)
    turned = (heads, dim, tokens)
    links = (far, rows, dim)
    dma = pltpu.SemaphoreType.DMA
    return pl.pallas_call(
        functools.partial(kernel, n_ctx, n_heads, chunks),
        out_shape=[jax.ShapeDtypeStruct(queries.shape, BF16)] * 4
        + [jax.ShapeDtypeStruct(level_weights.shape, F32)],
        in_specs=[vmem] * 6,
        out_specs=[vmem] * 5,
        scratch_shapes=[
            pltpu.VMEM((tokens, tokens), jnp.int32),
            pltpu.VMEM(turned, BF16),
            pltpu.VMEM(square, F32),
            pltpu.VMEM(square, F32),
            pltpu.VMEM(square, BF16),
            pltpu.VMEM((heads, far * dim, tokens), BF16),
            pltpu.VMEM(turned, F32),
            pltpu.VMEM(turned, F32),
            pltpu.VMEM(turned, BF16),
            pltpu.VMEM((heads, far * dim, dim), BF16),
            pltpu.VMEM(queries.shape, F32),
            pltpu.VMEM(queries.shape, F32),
        ]
        + [pltpu.VMEM(links, F32)] * 7
        + [pltpu.VMEM((8, tokens), F32), pltpu.VMEM((n_heads, 8, tokens), F32)]
        + [dma((far, chunks))] * 8
        + [dma((n_heads,))] * 2,
        compiler_params=pltpu.CompilerParams(
            collective_id=0, has_side_effects=True, vmem_limit_bytes=48 * 2**20
        ),
    )(queries, key_rows, value_rows, level_weights, norm_gain, grad_normed)


def solution(mesh):
    token_spec = P("heads", "ctx", None)
    in_specs = (token_spec,) * 3 + (P("heads", None, "ctx"), P("heads", None), token_spec)
    out_specs = (token_spec,) * 4 + (P("heads", None, "ctx"),)
    body = functools.partial(shards, mesh.shape["ctx"], mesh.shape["heads"])
    return jax.shard_map(body, mesh=mesh, in_specs=in_specs, out_specs=out_specs, check_vma=False)
```

```python
import functools
import math

import jax
import jax.numpy as jnp
from jax import lax
from jax.experimental import pallas as pl
from jax.experimental.pallas import tpu as pltpu
from jax.sharding import PartitionSpec as P

EPS = 1e-06
MESH = pl.DeviceIdType.MESH
F32 = jnp.float32
BF16 = jnp.bfloat16


def level_scale(number, head_dim):
    return 2.0 ** (-max(number - 1, 0) / 2.0) / math.sqrt(head_dim)


def dot(a, b):
    return jnp.dot(a, b, preferred_element_type=F32)


def dot_nt(a, b):
    return lax.dot_general(a, b, (((1,), (1,)), ((), ())), preferred_element_type=F32)


def kernel(
    n_ctx, n_heads, chunks,
    q_in, k_in, v_in, lw_in, gain_in, gn_in,
    normed_ref, gq_ref, gk_ref, gv_ref, glw_ref,
    q_ref, k_ref, v_ref, lw_ref, gain_ref, gn_ref, in_sem,
    bucket_ref, qt_ref, scores_ref, weights_ref, weighted_ref, sq_ref, att_ref, scaled_ref, gt_ref,
    states_ref, gk_acc, gv_acc,
    gsum, rcv, gs, rs, tx, brcv, abuf, hx, hx_in,
    fs_sem, fr_sem, gas_sem, gar_sem, rss_sem, rsr_sem, bs_sem, br_sem, hs_sem, hr_sem,
):
    heads, tokens, dim = q_ref.shape
    far = n_ctx.bit_length() - 1
    local = tokens.bit_length()
    width = heads * n_heads * dim
    rows = heads * dim
    part = rows // chunks
    per_chunk = heads // chunks
    me = lax.axis_index("ctx")
    mine = lax.axis_index("heads")
    bits = [(me // 2**i) % 2 for i in range(far)]

    def peer(j):
        other = me
        for i in range(far):
            if j >> i & 1:
                other = other + (1 - 2 * bits[i]) * 2**i
        return other

    def peer_bits(j):
        return [1 - bits[i] if j >> i & 1 else bits[i] for i in range(far)]

    def place(which, m, c):
        start = c * part
        for i in range(m):
            start = start + which[i] * (part >> (i + 1))
        return start

    def span(start, size):
        return pl.ds(pl.multiple_of(start, 8), size)

    pairs = ((k_in, k_ref), (v_in, v_ref), (q_in, q_ref), (lw_in, lw_ref), (gain_in, gain_ref), (gn_in, gn_ref))
    loads = [pltpu.make_async_copy(src, dst, in_sem.at[i]) for i, (src, dst) in enumerate(pairs)]
    for load in loads:
        load.start()

    barrier = pltpu.get_barrier_semaphore()
    friends = list(range(1, n_ctx // 2)) + [n_ctx // 2]
    for j in friends:
        pl.semaphore_signal(barrier, inc=1, device_id={"ctx": peer(j)}, device_id_type=MESH)
    for j in range(1, n_heads):
        pl.semaphore_signal(
            barrier, inc=1, device_id={"heads": (mine + j) % n_heads}, device_id_type=MESH
        )

    def key_value(h):
        gsum[0, h * dim : (h + 1) * dim, :] = dot(k_ref[h].T, v_ref[h])

    def remote(src, dst, ssem, rsem, target, axis="ctx"):
        return pltpu.make_async_remote_copy(
            src_ref=src, dst_ref=dst, send_sem=ssem, recv_sem=rsem,
            device_id={axis: target}, device_id_type=MESH,
        )

    def fwd_copy(m, c):
        where = span(place(bits, m, c), part >> m)
        return remote(
            gsum.at[m, where, :], rcv.at[m, where, :], fs_sem.at[m, c], fr_sem.at[m, c], peer(2**m)
        )

    def gather_copies(m, c):
        where = span(place(bits, m, c), part >> m)
        return [
            remote(rcv.at[m, where, :], rcv.at[m, where, :], gas_sem.at[m, c], gar_sem.at[m, c], peer(j))
            for j in range(1, 2**m)
        ]

    def fwd_step(m, c):
        fwd_copy(m, c).wait_recv()
        if m < far - 1:
            half = span(place(bits, m + 1, c), part >> (m + 1))
            gsum[m + 1, half, :] = gsum[m, half, :] + rcv[m, half, :]
            fwd_copy(m + 1, c).start()
        if m > 0:

            @pl.when(bits[m] == 1)
            def _():
                for copy in gather_copies(m, c):
                    copy.start()

    def gather_rows(m):
        return part - (part >> m)

    def local_wait(buffer, count, sem):
        pltpu.make_async_copy(buffer.at[pl.ds(0, count), :], buffer.at[pl.ds(0, count), :], sem).wait()

    s_pos = lax.broadcasted_iota(jnp.int32, (tokens, tokens), 0)
    t_pos = lax.broadcasted_iota(jnp.int32, (tokens, tokens), 1)

    def make_bucket():
        differ = jnp.bitwise_xor(s_pos, t_pos)
        bucket = jnp.zeros((tokens, tokens), jnp.int32)
        for exponent in range(local - 1):
            bucket = bucket + (differ >= 2**exponent).astype(jnp.int32)
        bucket_ref[...] = jnp.where(s_pos <= t_pos, bucket, -1)

    def near_forward(h):
        q_t = q_ref[h].T
        qt_ref[h] = q_t
        scores = dot(k_ref[h], q_t)
        scores_ref[h] = scores
        bucket = bucket_ref[...]
        weights = jnp.zeros((tokens, tokens), F32)
        for number in range(local):
            row = lw_ref[number, h : h + 1, :] * level_scale(number, dim)
            weights = jnp.where(bucket == number, row, weights)
        weights_ref[h] = weights
        weighted = (weights * scores).astype(BF16)
        weighted_ref[h] = weighted
        q_wide = q_t.astype(F32)
        for m in range(far):
            row = lw_ref[local + m, h : h + 1, :] * level_scale(local + m, dim)
            sq_ref[h, m * dim : (m + 1) * dim, :] = (row * q_wide).astype(BF16)
        att_ref[h] = dot(v_ref[h].T, weighted)
        gain = jnp.broadcast_to(gain_ref[h : h + 1, :], (tokens, dim))
        scaled_ref[h] = (gain * gn_ref[h].astype(F32)).T

    loads[0].wait()
    loads[1].wait()
    for h in range(per_chunk):
        key_value(h)
    pl.semaphore_wait(barrier, len(friends) + n_heads - 1)
    for c in range(chunks):
        if c > 0:
            for h in range(c * per_chunk, (c + 1) * per_chunk):
                key_value(h)
        fwd_copy(0, c).start()
    make_bucket()
    for load in loads[2:]:
        load.wait()
    pending = list(range(heads))
    near_forward(pending.pop(0))
    for t in range(far + chunks - 1):
        for c in range(chunks):
            if 0 <= t - c < far:
                fwd_step(t - c, c)
        if pending:
            near_forward(pending.pop(0))
    while pending:
        near_forward(pending.pop(0))
    for m in range(far):

        @pl.when(bits[m] == 1)
        def _():
            for c in range(chunks):
                if m > 0:
                    local_wait(rcv.at[m], gather_rows(m), gar_sem.at[m, c])
            for h in range(heads):
                states_ref[h, m * dim : (m + 1) * dim, :] = rcv[m, h * dim : (h + 1) * dim, :].astype(BF16)

        @pl.when(bits[m] == 0)
        def _():
            for h in range(heads):
                states_ref[h, m * dim : (m + 1) * dim, :] = jnp.zeros((dim, dim), BF16)

    total = jnp.zeros((1, tokens), F32)
    inner = jnp.zeros((1, tokens), F32)
    for h in range(heads):
        att = att_ref[h] + dot(states_ref[h].T, sq_ref[h])
        att_ref[h] = att
        total = total + jnp.sum(att * att, axis=0, keepdims=True)
        inner = inner + jnp.sum(att * scaled_ref[h], axis=0, keepdims=True)
    hx[0:1, :] = total
    hx[1:2, :] = inner
    head_copies = [
        remote(hx, hx_in.at[j], hs_sem.at[j], hr_sem.at[j], (mine + j) % n_heads, "heads")
        for j in range(1, n_heads)
    ]
    for copy in head_copies:
        copy.start()
    for j, copy in enumerate(head_copies):
        copy.wait_recv()
        total = total + hx_in[j + 1, 0:1, :]
        inner = inner + hx_in[j + 1, 1:2, :]
    inv_rms = lax.rsqrt(total / width + EPS)
    pull = inv_rms * inv_rms * inv_rms * inner / width

    def scatter_copies(m, c):
        size = part >> m
        copies = []
        for j in range(1, 2**m):
            where = span(place(peer_bits(j), m, c), size)
            slot = pl.ds(j * chunks * size + c * size, size)
            copies.append(
                remote(gs.at[m, where, :], rs.at[m, slot, :], rss_sem.at[m, c], rsr_sem.at[m, c], peer(j))
            )
        return copies

    def up_copy(m, c):
        where = span(place(bits, m, c), part >> m)
        return remote(tx.at[m, where, :], brcv.at[m, where, :], bs_sem.at[m, c], br_sem.at[m, c], peer(2**m))

    def down_copy(m, c):
        where = span(place(bits[:m] + [0], m + 1, c), part >> (m + 1))
        return remote(
            abuf.at[m + 1, where, :], brcv.at[m, where, :], bs_sem.at[m, c], br_sem.at[m, c], peer(2**m)
        )

    def bwd_send(m, c):
        size = part >> m

        @pl.when(bits[m] == 1)
        def _():
            where = span(place(bits, m, c), size)
            sums = gs[m, where, :]
            if m > 0:
                local_wait(rs.at[m], gather_rows(m), rsr_sem.at[m, c])
                for j in range(1, 2**m):
                    slot = j * chunks * size + c * size
                    sums = sums + rs[m, slot : slot + size, :]
            tx[m, where, :] = sums
            if m < far - 1:
                half = span(place(bits[:m] + [1], m + 1, c), size // 2)
                tx[m, half, :] = tx[m, half, :] + abuf[m + 1, half, :]
            up_copy(m, c).start()

        if m < far - 1:

            @pl.when(bits[m] == 0)
            def _():
                down_copy(m, c).start()

    def bwd_recv(m, c):
        size = part >> m
        half0 = span(place(bits[:m] + [0], m + 1, c), size // 2)
        half1 = span(place(bits[:m] + [1], m + 1, c), size // 2)

        @pl.when(bits[m] == 0)
        def _():
            up_copy(m, c).wait_recv()
            low = brcv[m, half0, :]
            if m < far - 1:
                low = low + abuf[m + 1, half0, :]
            abuf[m, half0, :] = low
            abuf[m, half1, :] = brcv[m, half1, :]

        @pl.when(bits[m] == 1)
        def _():
            if m < far - 1:
                down_copy(m, c).wait_recv()
                abuf[m, half0, :] = brcv[m, half0, :]
                abuf[m, half1, :] = abuf[m + 1, half1, :]
            else:
                abuf[m, half0, :] = jnp.zeros((size // 2, dim), F32)
                abuf[m, half1, :] = jnp.zeros((size // 2, dim), F32)

    for c in range(chunks):
        for h in range(c * per_chunk, (c + 1) * per_chunk):
            g_t = (inv_rms * scaled_ref[h] - att_ref[h] * pull).astype(BF16)
            gt_ref[h] = g_t
            grads = dot_nt(sq_ref[h], g_t)
            for m in range(far):
                gs[m, h * dim : (h + 1) * dim, :] = grads[m * dim : (m + 1) * dim, :]
        for m in reversed(range(1, far)):

            @pl.when(bits[m] == 1)
            def _():
                for copy in scatter_copies(m, c):
                    copy.start()

    def near_backward(h):
        gain = jnp.broadcast_to(gain_ref[h : h + 1, :], (tokens, dim))
        normed_ref[h] = ((att_ref[h] * inv_rms).T * gain).astype(BF16)
        g_t = gt_ref[h]
        mix = dot(v_ref[h], g_t)
        grad_scores = (weights_ref[h] * mix).astype(BF16)
        product = mix * scores_ref[h]
        bucket = bucket_ref[...]
        for number in range(local):
            kept = jnp.where(bucket == number, product, 0.0)
            glw_ref[number, h : h + 1, :] = level_scale(number, dim) * jnp.sum(kept, axis=0, keepdims=True)
        grad_q = dot(k_ref[h].T, grad_scores)
        turned = dot(states_ref[h], g_t)
        q_wide = qt_ref[h].astype(F32)
        for m in range(far):
            block = turned[m * dim : (m + 1) * dim, :]
            scale = level_scale(local + m, dim)
            glw_ref[local + m, h : h + 1, :] = scale * jnp.sum(block * q_wide, axis=0, keepdims=True)
            grad_q = grad_q + (lw_ref[local + m, h : h + 1, :] * scale) * block
        gq_ref[h] = grad_q.T.astype(BF16)
        gk_acc[h] = dot_nt(grad_scores, qt_ref[h])
        gv_acc[h] = dot_nt(weighted_ref[h], g_t)

    pending = list(range(heads))
    near_backward(pending.pop(0))
    for t in range(far + chunks):
        for c in range(chunks):
            stage = t - c
            if 1 <= stage <= far:
                bwd_recv(far - stage, c)
                if stage == far:
                    for h in range(c * per_chunk, (c + 1) * per_chunk):
                        while h in pending:
                            near_backward(pending.pop(0))
                        grad_kv = abuf[0, h * dim : (h + 1) * dim, :].astype(BF16)
                        gk_ref[h] = (gk_acc[h] + dot_nt(v_ref[h], grad_kv)).astype(BF16)
                        gv_ref[h] = (gv_acc[h] + dot(k_ref[h], grad_kv)).astype(BF16)
            if 0 <= stage < far:
                bwd_send(far - 1 - stage, c)
        if pending:
            near_backward(pending.pop(0))

    for copy in head_copies:
        copy.wait_send()
    for c in range(chunks):
        for m in range(far):
            fwd_copy(m, c).wait_send()

            @pl.when(bits[m] == 1)
            def _():
                if m > 0:
                    local_wait(rcv.at[m], gather_rows(m), gas_sem.at[m, c])
                    local_wait(gs.at[m], gather_rows(m), rss_sem.at[m, c])
                up_copy(m, c).wait_send()

            if m < far - 1:

                @pl.when(bits[m] == 0)
                def _():
                    down_copy(m, c).wait_send()


def put_out(*refs):
    copies = [pltpu.make_async_copy(refs[i], refs[5 + i], refs[10].at[i]) for i in range(5)]
    for copy in copies:
        copy.start()
    for copy in copies:
        copy.wait()


def shards(n_ctx, n_heads, queries, key_rows, value_rows, level_weights, norm_gain, grad_normed):
    heads, tokens, dim = queries.shape
    far = n_ctx.bit_length() - 1
    rows = heads * dim
    chunks = 1
    vmem = pl.BlockSpec(memory_space=pltpu.VMEM)
    square = (heads, tokens, tokens)
    turned = (heads, dim, tokens)
    links = (far, rows, dim)
    dma = pltpu.SemaphoreType.DMA
    rates = jnp.transpose(level_weights, (1, 0, 2))
    results = pl.pallas_call(
        functools.partial(kernel, n_ctx, n_heads, chunks),
        out_shape=[jax.ShapeDtypeStruct(queries.shape, BF16)] * 4
        + [jax.ShapeDtypeStruct(rates.shape, F32)],
        in_specs=[pl.BlockSpec(memory_space=pltpu.HBM)] * 6,
        out_specs=[vmem] * 5,
        scratch_shapes=[
            pltpu.VMEM(queries.shape, BF16),
            pltpu.VMEM(queries.shape, BF16),
            pltpu.VMEM(queries.shape, BF16),
            pltpu.VMEM(rates.shape, F32),
            pltpu.VMEM(norm_gain.shape, F32),
            pltpu.VMEM(queries.shape, BF16),
            dma((6,)),
            pltpu.VMEM((tokens, tokens), jnp.int32),
            pltpu.VMEM(turned, BF16),
            pltpu.VMEM(square, F32),
            pltpu.VMEM(square, F32),
            pltpu.VMEM(square, BF16),
            pltpu.VMEM((heads, far * dim, tokens), BF16),
            pltpu.VMEM(turned, F32),
            pltpu.VMEM(turned, F32),
            pltpu.VMEM(turned, BF16),
            pltpu.VMEM((heads, far * dim, dim), BF16),
            pltpu.VMEM(queries.shape, F32),
            pltpu.VMEM(queries.shape, F32),
        ]
        + [pltpu.VMEM(links, F32)] * 7
        + [pltpu.VMEM((8, tokens), F32), pltpu.VMEM((n_heads, 8, tokens), F32)]
        + [dma((far, chunks))] * 8
        + [dma((n_heads,))] * 2,
        compiler_params=pltpu.CompilerParams(
            collective_id=0, has_side_effects=True, vmem_limit_bytes=48 * 2**20
        ),
    )(queries, key_rows, value_rows, rates, norm_gain, grad_normed)
    results = pl.pallas_call(
        put_out,
        out_shape=[jax.ShapeDtypeStruct(x.shape, x.dtype) for x in results],
        in_specs=[pl.BlockSpec(memory_space=pl.ANY)] * 5,
        out_specs=[pl.BlockSpec(memory_space=pltpu.HBM)] * 5,
        scratch_shapes=[dma((5,))],
        compiler_params=pltpu.CompilerParams(vmem_limit_bytes=2**20),
    )(*results)
    return (*results[:4], jnp.transpose(results[4], (1, 0, 2)))


def solution(mesh):
    token_spec = P("heads", "ctx", None)
    in_specs = (token_spec,) * 3 + (P("heads", None, "ctx"), P("heads", None), token_spec)
    out_specs = (token_spec,) * 4 + (P("heads", None, "ctx"),)
    body = functools.partial(shards, mesh.shape["ctx"], mesh.shape["heads"])
    return jax.shard_map(body, mesh=mesh, in_specs=in_specs, out_specs=out_specs, check_vma=False)
```

```python
import functools
import math

import jax
import jax.numpy as jnp
from jax import lax
from jax.experimental import pallas as pl
from jax.experimental.pallas import tpu as pltpu
from jax.sharding import PartitionSpec as P

EPS = 1e-06
MESH = pl.DeviceIdType.MESH
F32 = jnp.float32
BF16 = jnp.bfloat16


def level_scale(number, head_dim):
    return 2.0 ** (-max(number - 1, 0) / 2.0) / math.sqrt(head_dim)


def dot(a, b):
    return jnp.dot(a, b, preferred_element_type=F32)


def dot_nt(a, b):
    return lax.dot_general(a, b, (((1,), (1,)), ((), ())), preferred_element_type=F32)


def kernel(
    n_ctx, n_heads, chunks,
    q_in, k_in, v_in, lw_in, gain_in, gn_in,
    normed_ref, gq_ref, gk_ref, gv_ref, glw_ref,
    q_ref, k_ref, v_ref, lw_ref, gain_ref, gn_ref, in_sem,
    bucket_ref, qt_ref, scores_ref, weights_ref, weighted_ref, sq_ref, att_ref, scaled_ref, gt_ref,
    states_ref, gk_acc, gv_acc,
    gsum, rcv, gs, rs, tx, brcv, abuf, hx, hx_in,
    fs_sem, fr_sem, gas_sem, gar_sem, rss_sem, rsr_sem, bs_sem, br_sem, hs_sem, hr_sem,
):
    heads, tokens, dim = q_ref.shape
    far = n_ctx.bit_length() - 1
    local = tokens.bit_length()
    width = heads * n_heads * dim
    rows = heads * dim
    part = rows // chunks
    per_chunk = heads // chunks
    me = lax.axis_index("ctx")
    mine = lax.axis_index("heads")
    bits = [(me // 2**i) % 2 for i in range(far)]

    def peer(j):
        other = me
        for i in range(far):
            if j >> i & 1:
                other = other + (1 - 2 * bits[i]) * 2**i
        return other

    def peer_bits(j):
        return [1 - bits[i] if j >> i & 1 else bits[i] for i in range(far)]

    def place(which, m, c):
        start = c * part
        for i in range(m):
            start = start + which[i] * (part >> (i + 1))
        return start

    def span(start, size):
        return pl.ds(pl.multiple_of(start, 8), size)

    pairs = ((k_in, k_ref), (v_in, v_ref), (q_in, q_ref), (lw_in, lw_ref), (gain_in, gain_ref), (gn_in, gn_ref))
    loads = [pltpu.make_async_copy(src, dst, in_sem.at[i]) for i, (src, dst) in enumerate(pairs)]
    for load in loads:
        load.start()

    barrier = pltpu.get_barrier_semaphore()
    friends = list(range(1, n_ctx // 2)) + [n_ctx // 2]
    for j in friends:
        pl.semaphore_signal(barrier, inc=1, device_id={"ctx": peer(j)}, device_id_type=MESH)
    for j in range(1, n_heads):
        pl.semaphore_signal(
            barrier, inc=1, device_id={"heads": (mine + j) % n_heads}, device_id_type=MESH
        )

    def key_value(h):
        gsum[0, h * dim : (h + 1) * dim, :] = dot(k_ref[h].T, v_ref[h])

    def remote(src, dst, ssem, rsem, target, axis="ctx"):
        return pltpu.make_async_remote_copy(
            src_ref=src, dst_ref=dst, send_sem=ssem, recv_sem=rsem,
            device_id={axis: target}, device_id_type=MESH,
        )

    def fwd_copy(m, c):
        where = span(place(bits, m, c), part >> m)
        return remote(
            gsum.at[m, where, :], rcv.at[m, where, :], fs_sem.at[m, c], fr_sem.at[m, c], peer(2**m)
        )

    def gather_copies(m, c):
        where = span(place(bits, m, c), part >> m)
        return [
            remote(rcv.at[m, where, :], rcv.at[m, where, :], gas_sem.at[m, c], gar_sem.at[m, c], peer(j))
            for j in range(1, 2**m)
        ]

    def fwd_step(m, c):
        fwd_copy(m, c).wait_recv()
        if m < far - 1:
            half = span(place(bits, m + 1, c), part >> (m + 1))
            gsum[m + 1, half, :] = gsum[m, half, :] + rcv[m, half, :]
            fwd_copy(m + 1, c).start()
        if m > 0:

            @pl.when(bits[m] == 1)
            def _():
                for copy in gather_copies(m, c):
                    copy.start()

    def gather_rows(m):
        return part - (part >> m)

    def local_wait(buffer, count, sem):
        pltpu.make_async_copy(buffer.at[pl.ds(0, count), :], buffer.at[pl.ds(0, count), :], sem).wait()

    s_pos = lax.broadcasted_iota(jnp.int32, (tokens, tokens), 0)
    t_pos = lax.broadcasted_iota(jnp.int32, (tokens, tokens), 1)

    def make_bucket():
        differ = jnp.bitwise_xor(s_pos, t_pos)
        bucket = jnp.zeros((tokens, tokens), jnp.int32)
        for exponent in range(local - 1):
            bucket = bucket + (differ >= 2**exponent).astype(jnp.int32)
        bucket_ref[...] = jnp.where(s_pos <= t_pos, bucket, -1)

    def near_forward(h):
        q_t = q_ref[h].T
        qt_ref[h] = q_t
        scores = dot(k_ref[h], q_t)
        scores_ref[h] = scores
        bucket = bucket_ref[...]
        weights = jnp.zeros((tokens, tokens), F32)
        for number in range(local):
            row = lw_ref[number, h : h + 1, :] * level_scale(number, dim)
            weights = jnp.where(bucket == number, row, weights)
        weights_ref[h] = weights
        weighted = (weights * scores).astype(BF16)
        weighted_ref[h] = weighted
        q_wide = q_t.astype(F32)
        for m in range(far):
            row = lw_ref[local + m, h : h + 1, :] * level_scale(local + m, dim)
            sq_ref[h, m * dim : (m + 1) * dim, :] = (row * q_wide).astype(BF16)
        att_ref[h] = dot(v_ref[h].T, weighted)
        gain = jnp.broadcast_to(gain_ref[h : h + 1, :], (tokens, dim))
        scaled_ref[h] = (gain * gn_ref[h].astype(F32)).T

    loads[0].wait()
    loads[1].wait()
    for h in range(per_chunk):
        key_value(h)
    pl.semaphore_wait(barrier, len(friends) + n_heads - 1)
    for c in range(chunks):
        if c > 0:
            for h in range(c * per_chunk, (c + 1) * per_chunk):
                key_value(h)
        fwd_copy(0, c).start()
    make_bucket()
    for load in loads[2:]:
        load.wait()
    pending = list(range(heads))
    near_forward(pending.pop(0))
    for t in range(far + chunks - 1):
        for c in range(chunks):
            if 0 <= t - c < far:
                fwd_step(t - c, c)
        if pending:
            near_forward(pending.pop(0))
    while pending:
        near_forward(pending.pop(0))
    for m in range(far):

        @pl.when(bits[m] == 1)
        def _():
            for c in range(chunks):
                if m > 0:
                    local_wait(rcv.at[m], gather_rows(m), gar_sem.at[m, c])
            for h in range(heads):
                states_ref[h, m * dim : (m + 1) * dim, :] = rcv[m, h * dim : (h + 1) * dim, :].astype(BF16)

        @pl.when(bits[m] == 0)
        def _():
            for h in range(heads):
                states_ref[h, m * dim : (m + 1) * dim, :] = jnp.zeros((dim, dim), BF16)

    total = jnp.zeros((1, tokens), F32)
    inner = jnp.zeros((1, tokens), F32)
    for h in range(heads):
        att = att_ref[h] + dot(states_ref[h].T, sq_ref[h])
        att_ref[h] = att
        total = total + jnp.sum(att * att, axis=0, keepdims=True)
        inner = inner + jnp.sum(att * scaled_ref[h], axis=0, keepdims=True)
    hx[0:1, :] = total
    hx[1:2, :] = inner
    head_copies = [
        remote(hx, hx_in.at[j], hs_sem.at[j], hr_sem.at[j], (mine + j) % n_heads, "heads")
        for j in range(1, n_heads)
    ]
    for copy in head_copies:
        copy.start()
    for j, copy in enumerate(head_copies):
        copy.wait_recv()
        total = total + hx_in[j + 1, 0:1, :]
        inner = inner + hx_in[j + 1, 1:2, :]
    inv_rms = lax.rsqrt(total / width + EPS)
    pull = inv_rms * inv_rms * inv_rms * inner / width

    def scatter_copies(m, c):
        size = part >> m
        copies = []
        for j in range(1, 2**m):
            where = span(place(peer_bits(j), m, c), size)
            slot = pl.ds(j * chunks * size + c * size, size)
            copies.append(
                remote(gs.at[m, where, :], rs.at[m, slot, :], rss_sem.at[m, c], rsr_sem.at[m, c], peer(j))
            )
        return copies

    def up_copy(m, c):
        where = span(place(bits, m, c), part >> m)
        return remote(tx.at[m, where, :], brcv.at[m, where, :], bs_sem.at[m, c], br_sem.at[m, c], peer(2**m))

    def down_copy(m, c):
        where = span(place(bits[:m] + [0], m + 1, c), part >> (m + 1))
        return remote(
            abuf.at[m + 1, where, :], brcv.at[m, where, :], bs_sem.at[m, c], br_sem.at[m, c], peer(2**m)
        )

    def bwd_send(m, c):
        size = part >> m

        @pl.when(bits[m] == 1)
        def _():
            where = span(place(bits, m, c), size)
            sums = gs[m, where, :]
            if m > 0:
                local_wait(rs.at[m], gather_rows(m), rsr_sem.at[m, c])
                for j in range(1, 2**m):
                    slot = j * chunks * size + c * size
                    sums = sums + rs[m, slot : slot + size, :]
            tx[m, where, :] = sums
            if m < far - 1:
                half = span(place(bits[:m] + [1], m + 1, c), size // 2)
                tx[m, half, :] = tx[m, half, :] + abuf[m + 1, half, :]
            up_copy(m, c).start()

        if m < far - 1:

            @pl.when(bits[m] == 0)
            def _():
                down_copy(m, c).start()

    def bwd_recv(m, c):
        size = part >> m
        half0 = span(place(bits[:m] + [0], m + 1, c), size // 2)
        half1 = span(place(bits[:m] + [1], m + 1, c), size // 2)

        @pl.when(bits[m] == 0)
        def _():
            up_copy(m, c).wait_recv()
            low = brcv[m, half0, :]
            if m < far - 1:
                low = low + abuf[m + 1, half0, :]
            abuf[m, half0, :] = low
            abuf[m, half1, :] = brcv[m, half1, :]

        @pl.when(bits[m] == 1)
        def _():
            if m < far - 1:
                down_copy(m, c).wait_recv()
                abuf[m, half0, :] = brcv[m, half0, :]
                abuf[m, half1, :] = abuf[m + 1, half1, :]
            else:
                abuf[m, half0, :] = jnp.zeros((size // 2, dim), F32)
                abuf[m, half1, :] = jnp.zeros((size // 2, dim), F32)

    for c in range(chunks):
        for h in range(c * per_chunk, (c + 1) * per_chunk):
            g_t = (inv_rms * scaled_ref[h] - att_ref[h] * pull).astype(BF16)
            gt_ref[h] = g_t
            grads = dot_nt(sq_ref[h], g_t)
            for m in range(far):
                gs[m, h * dim : (h + 1) * dim, :] = grads[m * dim : (m + 1) * dim, :]
        for m in reversed(range(1, far)):

            @pl.when(bits[m] == 1)
            def _():
                for copy in scatter_copies(m, c):
                    copy.start()

    def near_backward(h):
        gain = jnp.broadcast_to(gain_ref[h : h + 1, :], (tokens, dim))
        normed_ref[h] = ((att_ref[h] * inv_rms).T * gain).astype(BF16)
        g_t = gt_ref[h]
        mix = dot(v_ref[h], g_t)
        grad_scores = (weights_ref[h] * mix).astype(BF16)
        product = mix * scores_ref[h]
        bucket = bucket_ref[...]
        for number in range(local):
            kept = jnp.where(bucket == number, product, 0.0)
            glw_ref[number, h : h + 1, :] = level_scale(number, dim) * jnp.sum(kept, axis=0, keepdims=True)
        grad_q = dot(k_ref[h].T, grad_scores)
        turned = dot(states_ref[h], g_t)
        q_wide = qt_ref[h].astype(F32)
        for m in range(far):
            block = turned[m * dim : (m + 1) * dim, :]
            scale = level_scale(local + m, dim)
            glw_ref[local + m, h : h + 1, :] = scale * jnp.sum(block * q_wide, axis=0, keepdims=True)
            grad_q = grad_q + (lw_ref[local + m, h : h + 1, :] * scale) * block
        gq_ref[h] = grad_q.T.astype(BF16)
        gk_acc[h] = dot_nt(grad_scores, qt_ref[h])
        gv_acc[h] = dot_nt(weighted_ref[h], g_t)

    pending = list(range(heads))
    near_backward(pending.pop(0))
    for t in range(far + chunks):
        for c in range(chunks):
            stage = t - c
            if 1 <= stage <= far:
                bwd_recv(far - stage, c)
                if stage == far:
                    for h in range(c * per_chunk, (c + 1) * per_chunk):
                        while h in pending:
                            near_backward(pending.pop(0))
                        grad_kv = abuf[0, h * dim : (h + 1) * dim, :].astype(BF16)
                        gk_ref[h] = (gk_acc[h] + dot_nt(v_ref[h], grad_kv)).astype(BF16)
                        gv_ref[h] = (gv_acc[h] + dot(k_ref[h], grad_kv)).astype(BF16)
            if 0 <= stage < far:
                bwd_send(far - 1 - stage, c)
        if pending:
            near_backward(pending.pop(0))

    for copy in head_copies:
        copy.wait_send()
    for c in range(chunks):
        for m in range(far):
            fwd_copy(m, c).wait_send()

            @pl.when(bits[m] == 1)
            def _():
                if m > 0:
                    local_wait(rcv.at[m], gather_rows(m), gas_sem.at[m, c])
                    local_wait(gs.at[m], gather_rows(m), rss_sem.at[m, c])
                up_copy(m, c).wait_send()

            if m < far - 1:

                @pl.when(bits[m] == 0)
                def _():
                    down_copy(m, c).wait_send()


def put_out(*refs):
    copies = [pltpu.make_async_copy(refs[i], refs[5 + i], refs[10].at[i]) for i in range(5)]
    for copy in copies:
        copy.start()
    for copy in copies:
        copy.wait()


def shards(n_ctx, n_heads, queries, key_rows, value_rows, level_weights, norm_gain, grad_normed):
    heads, tokens, dim = queries.shape
    far = n_ctx.bit_length() - 1
    rows = heads * dim
    chunks = 1
    vmem = pl.BlockSpec(memory_space=pltpu.VMEM)
    square = (heads, tokens, tokens)
    turned = (heads, dim, tokens)
    links = (far, rows, dim)
    dma = pltpu.SemaphoreType.DMA
    rates = jnp.transpose(level_weights, (1, 0, 2))
    results = pl.pallas_call(
        functools.partial(kernel, n_ctx, n_heads, chunks),
        out_shape=[jax.ShapeDtypeStruct(queries.shape, BF16)] * 4
        + [jax.ShapeDtypeStruct(rates.shape, F32)],
        in_specs=[pl.BlockSpec(memory_space=pltpu.HBM)] * 6,
        out_specs=[vmem] * 5,
        scratch_shapes=[
            pltpu.VMEM(queries.shape, BF16),
            pltpu.VMEM(queries.shape, BF16),
            pltpu.VMEM(queries.shape, BF16),
            pltpu.VMEM(rates.shape, F32),
            pltpu.VMEM(norm_gain.shape, F32),
            pltpu.VMEM(queries.shape, BF16),
            dma((6,)),
            pltpu.VMEM((tokens, tokens), jnp.int32),
            pltpu.VMEM(turned, BF16),
            pltpu.VMEM(square, F32),
            pltpu.VMEM(square, F32),
            pltpu.VMEM(square, BF16),
            pltpu.VMEM((heads, far * dim, tokens), BF16),
            pltpu.VMEM(turned, F32),
            pltpu.VMEM(turned, F32),
            pltpu.VMEM(turned, BF16),
            pltpu.VMEM((heads, far * dim, dim), BF16),
            pltpu.VMEM(queries.shape, F32),
            pltpu.VMEM(queries.shape, F32),
        ]
        + [pltpu.VMEM(links, F32)] * 7
        + [pltpu.VMEM((8, tokens), F32), pltpu.VMEM((n_heads, 8, tokens), F32)]
        + [dma((far, chunks))] * 8
        + [dma((n_heads,))] * 2,
        compiler_params=pltpu.CompilerParams(
            collective_id=0, has_side_effects=True, vmem_limit_bytes=48 * 2**20
        ),
    )(*[pltpu.with_memory_space_constraint(x, pltpu.HBM) for x in (queries, key_rows, value_rows, rates, norm_gain, grad_normed)])
    results = pl.pallas_call(
        put_out,
        out_shape=[jax.ShapeDtypeStruct(x.shape, x.dtype) for x in results],
        in_specs=[pl.BlockSpec(memory_space=pl.ANY)] * 5,
        out_specs=[pl.BlockSpec(memory_space=pltpu.HBM)] * 5,
        scratch_shapes=[dma((5,))],
        compiler_params=pltpu.CompilerParams(vmem_limit_bytes=2**20),
    )(*results)
    return (*results[:4], jnp.transpose(results[4], (1, 0, 2)))


def solution(mesh):
    token_spec = P("heads", "ctx", None)
    in_specs = (token_spec,) * 3 + (P("heads", None, "ctx"), P("heads", None), token_spec)
    out_specs = (token_spec,) * 4 + (P("heads", None, "ctx"),)
    body = functools.partial(shards, mesh.shape["ctx"], mesh.shape["heads"])
    return jax.shard_map(body, mesh=mesh, in_specs=in_specs, out_specs=out_specs, check_vma=False)
```

```python
import functools
import math

import jax
import jax.numpy as jnp
from jax import lax
from jax.experimental import pallas as pl
from jax.experimental.pallas import tpu as pltpu
from jax.sharding import PartitionSpec as P

EPS = 1e-06
MESH = pl.DeviceIdType.MESH
F32 = jnp.float32
BF16 = jnp.bfloat16


def level_scale(number, head_dim):
    return 2.0 ** (-max(number - 1, 0) / 2.0) / math.sqrt(head_dim)


def dot(a, b):
    return jnp.dot(a, b, preferred_element_type=F32)


def dot_nt(a, b):
    return lax.dot_general(a, b, (((1,), (1,)), ((), ())), preferred_element_type=F32)


def kernel(
    n_ctx, n_heads, chunks,
    q_in, k_in, v_in, lw_in, gain_in, gn_in,
    normed_ref, gq_ref, gk_ref, gv_ref, glw_ref,
    q_ref, k_ref, v_ref, lw_ref, gain_ref, gn_ref, in_sem,
    bucket_ref, qt_ref, scores_ref, weights_ref, weighted_ref, sq_ref, att_ref, scaled_ref, gt_ref,
    states_ref, gk_acc, gv_acc,
    gsum, rcv, gs, rs, tx, brcv, abuf, hx, hx_in,
    fs_sem, fr_sem, gas_sem, gar_sem, rss_sem, rsr_sem, bs_sem, br_sem, hs_sem, hr_sem,
):
    heads, tokens, dim = q_ref.shape
    far = n_ctx.bit_length() - 1
    local = tokens.bit_length()
    width = heads * n_heads * dim
    rows = heads * dim
    part = rows // chunks
    per_chunk = heads // chunks
    me = lax.axis_index("ctx")
    mine = lax.axis_index("heads")
    bits = [(me // 2**i) % 2 for i in range(far)]

    def peer(j):
        other = me
        for i in range(far):
            if j >> i & 1:
                other = other + (1 - 2 * bits[i]) * 2**i
        return other

    def peer_bits(j):
        return [1 - bits[i] if j >> i & 1 else bits[i] for i in range(far)]

    def place(which, m, c):
        start = c * part
        for i in range(m):
            start = start + which[i] * (part >> (i + 1))
        return start

    def span(start, size):
        return pl.ds(pl.multiple_of(start, 8), size)

    pairs = ((k_in, k_ref), (v_in, v_ref), (q_in, q_ref), (lw_in, lw_ref), (gain_in, gain_ref), (gn_in, gn_ref))
    loads = [pltpu.make_async_copy(src, dst, in_sem.at[i]) for i, (src, dst) in enumerate(pairs)]
    for load in loads:
        load.start()

    barrier = pltpu.get_barrier_semaphore()
    friends = list(range(1, n_ctx // 2)) + [n_ctx // 2]
    for j in friends:
        pl.semaphore_signal(barrier, inc=1, device_id={"ctx": peer(j)}, device_id_type=MESH)
    for j in range(1, n_heads):
        pl.semaphore_signal(
            barrier, inc=1, device_id={"heads": (mine + j) % n_heads}, device_id_type=MESH
        )

    def key_value(h):
        gsum[0, h * dim : (h + 1) * dim, :] = dot(k_ref[h].T, v_ref[h])

    def remote(src, dst, ssem, rsem, target, axis="ctx"):
        return pltpu.make_async_remote_copy(
            src_ref=src, dst_ref=dst, send_sem=ssem, recv_sem=rsem,
            device_id={axis: target}, device_id_type=MESH,
        )

    def fwd_copy(m, c):
        where = span(place(bits, m, c), part >> m)
        return remote(
            gsum.at[m, where, :], rcv.at[m, where, :], fs_sem.at[m, c], fr_sem.at[m, c], peer(2**m)
        )

    def gather_copies(m, c):
        where = span(place(bits, m, c), part >> m)
        return [
            remote(rcv.at[m, where, :], rcv.at[m, where, :], gas_sem.at[m, c], gar_sem.at[m, c], peer(j))
            for j in range(1, 2**m)
        ]

    def fwd_step(m, c):
        fwd_copy(m, c).wait_recv()
        if m < far - 1:
            half = span(place(bits, m + 1, c), part >> (m + 1))
            gsum[m + 1, half, :] = gsum[m, half, :] + rcv[m, half, :]
            fwd_copy(m + 1, c).start()
        if m > 0:

            @pl.when(bits[m] == 1)
            def _():
                for copy in gather_copies(m, c):
                    copy.start()

    def gather_rows(m):
        return part - (part >> m)

    def local_wait(buffer, count, sem):
        pltpu.make_async_copy(buffer.at[pl.ds(0, count), :], buffer.at[pl.ds(0, count), :], sem).wait()

    s_pos = lax.broadcasted_iota(jnp.int32, (tokens, tokens), 0)
    t_pos = lax.broadcasted_iota(jnp.int32, (tokens, tokens), 1)

    def make_bucket():
        differ = jnp.bitwise_xor(s_pos, t_pos)
        bucket = jnp.zeros((tokens, tokens), jnp.int32)
        for exponent in range(local - 1):
            bucket = bucket + (differ >= 2**exponent).astype(jnp.int32)
        bucket_ref[...] = jnp.where(s_pos <= t_pos, bucket, -1)

    def near_forward(h):
        q_t = q_ref[h].T
        qt_ref[h] = q_t
        scores = dot(k_ref[h], q_t)
        scores_ref[h] = scores
        bucket = bucket_ref[...]
        weights = jnp.zeros((tokens, tokens), F32)
        for number in range(local):
            row = lw_ref[number, h : h + 1, :] * level_scale(number, dim)
            weights = jnp.where(bucket == number, row, weights)
        weights_ref[h] = weights
        weighted = (weights * scores).astype(BF16)
        weighted_ref[h] = weighted
        q_wide = q_t.astype(F32)
        for m in range(far):
            row = lw_ref[local + m, h : h + 1, :] * level_scale(local + m, dim)
            sq_ref[h, m * dim : (m + 1) * dim, :] = (row * q_wide).astype(BF16)
        att_ref[h] = dot(v_ref[h].T, weighted)
        gain = jnp.broadcast_to(gain_ref[h : h + 1, :], (tokens, dim))
        scaled_ref[h] = (gain * gn_ref[h].astype(F32)).T

    loads[0].wait()
    loads[1].wait()
    for h in range(per_chunk):
        key_value(h)
    pl.semaphore_wait(barrier, len(friends) + n_heads - 1)
    for c in range(chunks):
        if c > 0:
            for h in range(c * per_chunk, (c + 1) * per_chunk):
                key_value(h)
        fwd_copy(0, c).start()
    make_bucket()
    for load in loads[2:]:
        load.wait()
    pending = list(range(heads))
    for t in range(far + chunks - 1):
        for c in range(chunks):
            if 0 <= t - c < far:
                fwd_step(t - c, c)
        if pending:
            near_forward(pending.pop(0))
    while pending:
        near_forward(pending.pop(0))
    for m in range(far):

        @pl.when(bits[m] == 1)
        def _():
            for c in range(chunks):
                if m > 0:
                    local_wait(rcv.at[m], gather_rows(m), gar_sem.at[m, c])
            for h in range(heads):
                states_ref[h, m * dim : (m + 1) * dim, :] = rcv[m, h * dim : (h + 1) * dim, :].astype(BF16)

        @pl.when(bits[m] == 0)
        def _():
            for h in range(heads):
                states_ref[h, m * dim : (m + 1) * dim, :] = jnp.zeros((dim, dim), BF16)

    total = jnp.zeros((1, tokens), F32)
    inner = jnp.zeros((1, tokens), F32)
    for h in range(heads):
        att = att_ref[h] + dot(states_ref[h].T, sq_ref[h])
        att_ref[h] = att
        total = total + jnp.sum(att * att, axis=0, keepdims=True)
        inner = inner + jnp.sum(att * scaled_ref[h], axis=0, keepdims=True)
    hx[0:1, :] = total
    hx[1:2, :] = inner
    head_copies = [
        remote(hx, hx_in.at[j], hs_sem.at[j], hr_sem.at[j], (mine + j) % n_heads, "heads")
        for j in range(1, n_heads)
    ]
    for copy in head_copies:
        copy.start()
    for j, copy in enumerate(head_copies):
        copy.wait_recv()
        total = total + hx_in[j + 1, 0:1, :]
        inner = inner + hx_in[j + 1, 1:2, :]
    inv_rms = lax.rsqrt(total / width + EPS)
    pull = inv_rms * inv_rms * inv_rms * inner / width

    def scatter_copies(m, c):
        size = part >> m
        copies = []
        for j in range(1, 2**m):
            where = span(place(peer_bits(j), m, c), size)
            slot = pl.ds(j * chunks * size + c * size, size)
            copies.append(
                remote(gs.at[m, where, :], rs.at[m, slot, :], rss_sem.at[m, c], rsr_sem.at[m, c], peer(j))
            )
        return copies

    def up_copy(m, c):
        where = span(place(bits, m, c), part >> m)
        return remote(tx.at[m, where, :], brcv.at[m, where, :], bs_sem.at[m, c], br_sem.at[m, c], peer(2**m))

    def down_copy(m, c):
        where = span(place(bits[:m] + [0], m + 1, c), part >> (m + 1))
        return remote(
            abuf.at[m + 1, where, :], brcv.at[m, where, :], bs_sem.at[m, c], br_sem.at[m, c], peer(2**m)
        )

    def bwd_send(m, c):
        size = part >> m

        @pl.when(bits[m] == 1)
        def _():
            where = span(place(bits, m, c), size)
            sums = gs[m, where, :]
            if m > 0:
                local_wait(rs.at[m], gather_rows(m), rsr_sem.at[m, c])
                for j in range(1, 2**m):
                    slot = j * chunks * size + c * size
                    sums = sums + rs[m, slot : slot + size, :]
            tx[m, where, :] = sums
            if m < far - 1:
                half = span(place(bits[:m] + [1], m + 1, c), size // 2)
                tx[m, half, :] = tx[m, half, :] + abuf[m + 1, half, :]
            up_copy(m, c).start()

        if m < far - 1:

            @pl.when(bits[m] == 0)
            def _():
                down_copy(m, c).start()

    def bwd_recv(m, c):
        size = part >> m
        half0 = span(place(bits[:m] + [0], m + 1, c), size // 2)
        half1 = span(place(bits[:m] + [1], m + 1, c), size // 2)

        @pl.when(bits[m] == 0)
        def _():
            up_copy(m, c).wait_recv()
            low = brcv[m, half0, :]
            if m < far - 1:
                low = low + abuf[m + 1, half0, :]
            abuf[m, half0, :] = low
            abuf[m, half1, :] = brcv[m, half1, :]

        @pl.when(bits[m] == 1)
        def _():
            if m < far - 1:
                down_copy(m, c).wait_recv()
                abuf[m, half0, :] = brcv[m, half0, :]
                abuf[m, half1, :] = abuf[m + 1, half1, :]
            else:
                abuf[m, half0, :] = jnp.zeros((size // 2, dim), F32)
                abuf[m, half1, :] = jnp.zeros((size // 2, dim), F32)

    for c in range(chunks):
        for h in range(c * per_chunk, (c + 1) * per_chunk):
            g_t = (inv_rms * scaled_ref[h] - att_ref[h] * pull).astype(BF16)
            gt_ref[h] = g_t
            grads = dot_nt(sq_ref[h], g_t)
            for m in range(far):
                gs[m, h * dim : (h + 1) * dim, :] = grads[m * dim : (m + 1) * dim, :]
        for m in reversed(range(1, far)):

            @pl.when(bits[m] == 1)
            def _():
                for copy in scatter_copies(m, c):
                    copy.start()

    def near_backward(h):
        gain = jnp.broadcast_to(gain_ref[h : h + 1, :], (tokens, dim))
        normed_ref[h] = ((att_ref[h] * inv_rms).T * gain).astype(BF16)
        g_t = gt_ref[h]
        mix = dot(v_ref[h], g_t)
        grad_scores = (weights_ref[h] * mix).astype(BF16)
        product = mix * scores_ref[h]
        bucket = bucket_ref[...]
        for number in range(local):
            kept = jnp.where(bucket == number, product, 0.0)
            glw_ref[number, h : h + 1, :] = level_scale(number, dim) * jnp.sum(kept, axis=0, keepdims=True)
        grad_q = dot(k_ref[h].T, grad_scores)
        turned = dot(states_ref[h], g_t)
        q_wide = qt_ref[h].astype(F32)
        for m in range(far):
            block = turned[m * dim : (m + 1) * dim, :]
            scale = level_scale(local + m, dim)
            glw_ref[local + m, h : h + 1, :] = scale * jnp.sum(block * q_wide, axis=0, keepdims=True)
            grad_q = grad_q + (lw_ref[local + m, h : h + 1, :] * scale) * block
        gq_ref[h] = grad_q.T.astype(BF16)
        gk_acc[h] = dot_nt(grad_scores, qt_ref[h])
        gv_acc[h] = dot_nt(weighted_ref[h], g_t)

    pending = list(range(heads))
    near_backward(pending.pop(0))
    for t in range(far + chunks):
        for c in range(chunks):
            stage = t - c
            if 1 <= stage <= far:
                bwd_recv(far - stage, c)
                if stage == far:
                    for h in range(c * per_chunk, (c + 1) * per_chunk):
                        while h in pending:
                            near_backward(pending.pop(0))
                        grad_kv = abuf[0, h * dim : (h + 1) * dim, :].astype(BF16)
                        gk_ref[h] = (gk_acc[h] + dot_nt(v_ref[h], grad_kv)).astype(BF16)
                        gv_ref[h] = (gv_acc[h] + dot(k_ref[h], grad_kv)).astype(BF16)
            if 0 <= stage < far:
                bwd_send(far - 1 - stage, c)
        if pending:
            near_backward(pending.pop(0))

    for copy in head_copies:
        copy.wait_send()
    for c in range(chunks):
        for m in range(far):
            fwd_copy(m, c).wait_send()

            @pl.when(bits[m] == 1)
            def _():
                if m > 0:
                    local_wait(rcv.at[m], gather_rows(m), gas_sem.at[m, c])
                    local_wait(gs.at[m], gather_rows(m), rss_sem.at[m, c])
                up_copy(m, c).wait_send()

            if m < far - 1:

                @pl.when(bits[m] == 0)
                def _():
                    down_copy(m, c).wait_send()


def put_out(*refs):
    copies = [pltpu.make_async_copy(refs[i], refs[5 + i], refs[10].at[i]) for i in range(5)]
    for copy in copies:
        copy.start()
    for copy in copies:
        copy.wait()


def shards(n_ctx, n_heads, queries, key_rows, value_rows, level_weights, norm_gain, grad_normed):
    heads, tokens, dim = queries.shape
    far = n_ctx.bit_length() - 1
    rows = heads * dim
    chunks = 1
    vmem = pl.BlockSpec(memory_space=pltpu.VMEM)
    square = (heads, tokens, tokens)
    turned = (heads, dim, tokens)
    links = (far, rows, dim)
    dma = pltpu.SemaphoreType.DMA
    rates = jnp.transpose(level_weights, (1, 0, 2))
    results = pl.pallas_call(
        functools.partial(kernel, n_ctx, n_heads, chunks),
        out_shape=[jax.ShapeDtypeStruct(queries.shape, BF16)] * 4
        + [jax.ShapeDtypeStruct(rates.shape, F32)],
        in_specs=[pl.BlockSpec(memory_space=pltpu.HBM)] * 6,
        out_specs=[vmem] * 5,
        scratch_shapes=[
            pltpu.VMEM(queries.shape, BF16),
            pltpu.VMEM(queries.shape, BF16),
            pltpu.VMEM(queries.shape, BF16),
            pltpu.VMEM(rates.shape, F32),
            pltpu.VMEM(norm_gain.shape, F32),
            pltpu.VMEM(queries.shape, BF16),
            dma((6,)),
            pltpu.VMEM((tokens, tokens), jnp.int32),
            pltpu.VMEM(turned, BF16),
            pltpu.VMEM(square, F32),
            pltpu.VMEM(square, F32),
            pltpu.VMEM(square, BF16),
            pltpu.VMEM((heads, far * dim, tokens), BF16),
            pltpu.VMEM(turned, F32),
            pltpu.VMEM(turned, F32),
            pltpu.VMEM(turned, BF16),
            pltpu.VMEM((heads, far * dim, dim), BF16),
            pltpu.VMEM(queries.shape, F32),
            pltpu.VMEM(queries.shape, F32),
        ]
        + [pltpu.VMEM(links, F32)] * 7
        + [pltpu.VMEM((8, tokens), F32), pltpu.VMEM((n_heads, 8, tokens), F32)]
        + [dma((far, chunks))] * 8
        + [dma((n_heads,))] * 2,
        compiler_params=pltpu.CompilerParams(
            collective_id=0, has_side_effects=True, vmem_limit_bytes=48 * 2**20
        ),
    )(*[pltpu.with_memory_space_constraint(x, pltpu.HBM) for x in (queries, key_rows, value_rows, rates, norm_gain, grad_normed)])
    results = pl.pallas_call(
        put_out,
        out_shape=[jax.ShapeDtypeStruct(x.shape, x.dtype) for x in results],
        in_specs=[pl.BlockSpec(memory_space=pl.ANY)] * 5,
        out_specs=[pl.BlockSpec(memory_space=pltpu.HBM)] * 5,
        scratch_shapes=[dma((5,))],
        compiler_params=pltpu.CompilerParams(vmem_limit_bytes=2**20),
    )(*results)
    return (*results[:4], jnp.transpose(results[4], (1, 0, 2)))


def solution(mesh):
    token_spec = P("heads", "ctx", None)
    in_specs = (token_spec,) * 3 + (P("heads", None, "ctx"), P("heads", None), token_spec)
    out_specs = (token_spec,) * 4 + (P("heads", None, "ctx"),)
    body = functools.partial(shards, mesh.shape["ctx"], mesh.shape["heads"])
    return jax.shard_map(body, mesh=mesh, in_specs=in_specs, out_specs=out_specs, check_vma=False)
```
